32 devices in a mesh: chars: 2 (over x), prow: 16 (over z, y, core).
Axes of the slice: x: 2, y: 2, z: 4, core: 2. Of those that a mesh axis runs over, the one named last changes fastest.
Arguments:
- queries: bfloat16 [8192, 512], P(('chars', 'prow')), parts along dimension 0, may hold values from -8 to 8
- keys: bfloat16 [8192, 512], P(('chars', 'prow')), parts along dimension 0, may hold values from -8 to 8
- values: bfloat16 [8192, 512], P(('chars', 'prow')), parts along dimension 0, may hold values from -6 to 6
- out_grad: bfloat16 [8192, 512], P(('chars', 'prow')), parts along dimension 0, may hold values from -6 to 6
- valid_counts: int32 [32, 4], P('chars'), parts along dimension 0, may hold values from 1 to 64
- landmark_cols: int32 [32], P('chars'), parts along dimension 0, may hold values from 0 to 3
- landmark_rows: int32 [32, 4], P(('chars', 'prow')), parts along dimension 0, may hold values from 0 to 15, as said below
Outputs:
- attn_out: bfloat16 [8192, 512], P(('chars', 'prow')), parts along dimension 0
- query_grad: bfloat16 [8192, 512], P(('chars', 'prow')), parts along dimension 0
- key_grad: bfloat16 [8192, 512], P(('chars', 'prow')), parts along dimension 0
- value_grad: bfloat16 [8192, 512], P(('chars', 'prow')), parts along dimension 0
The draws below stay inside these ranges and needn't reach their ends.
There are 2 independent parts, one for each index of `chars`. The reference program is written for one: setup_inputs(seed, part) draws one part's arguments, and reference() takes and returns one part's arrays. A program takes and returns all parts, laid end to end along the dimension named above; each array names one. Nothing has to cross between parts.
Inputs may be any that keep to these rules, and one draw needn't show every extreme that they name: `landmark_rows`: the 4 entries of each row are distinct.
All inputs are finite; a program needn't handle non-finite values.
Results may differ from the reference program's by a relative error of at most 0.012.
The reference program's roundings to bfloat16 on the way count: a program that leaves them out, or rounds other values in their place, can miss the bound.
Values may be sent and summed in bfloat16 or wider, within the bound.
A program may use at most 192 MiB of HBM per device.

```python
import math
import jax
import jax.numpy as jnp
from jax import lax

HEADS = 8
HD = 64
WIDTH = 512
BLK = 64
NLAND = 4
PC = 4
NROWS = 16
TOKENS = 4096


def drawn_field(key, member):
    base_key = jax.random.fold_in(key, 7 + member)
    drawn = jnp.clip(jax.random.normal(jax.random.fold_in(base_key, 2), (TOKENS, WIDTH)), -6.0, 6.0)
    return drawn.astype(jnp.bfloat16)


def draw_queries(key, part):
    return drawn_field(key, 0)


def draw_keys(key, part):
    return drawn_field(key, 1)


def draw_landmark_rows(key, part):
    row_keys = jax.vmap(lambda index: jax.random.fold_in(key, index))(jnp.arange(NROWS))
    orders = jax.vmap(lambda row_key: jax.random.permutation(row_key, NROWS))(row_keys)
    return orders[:, :NLAND].astype(jnp.int32)


def place_ends(values, rng, least, high):
    dims = values.shape
    place = [jax.random.randint(jax.random.fold_in(rng, axis), (), 0, dims[axis]) for axis in range(len(dims))]
    values = values.at[tuple(place)].set(least)
    longest = dims.index(max(dims))
    place[longest] = (place[longest] + 1) % dims[longest]
    return values.at[tuple(place)].set(high)


def block_scale(key, dims, cuts, least, largest):
    level = 1.0
    for axis_at, parts in cuts:
        heights = jax.random.uniform(jax.random.fold_in(jax.random.fold_in(key, 6), axis_at), (parts,), jnp.float32, least / len(cuts), largest / len(cuts))
        level = level * jnp.repeat(jnp.exp(heights), dims[axis_at] // parts).reshape((-1,) + (1,) * (len(dims) - 1 - axis_at))
    return level


def normal_values(key, extent, deviation, bound, shards=(), kind=jnp.bfloat16):
    entries = deviation * jax.random.normal(key, extent, jnp.float32)
    if shards:
        entries = entries * block_scale(key, extent, shards, -0.22, 0.18)
    return jnp.clip(entries, -bound, bound).astype(kind)


def setup_inputs(seed: int = 0, part: int = 0) -> dict:
    arg_keys = jax.random.split(jax.random.key(seed), 8)
    own_keys = jax.random.split(jax.random.fold_in(arg_keys[7], part), 8)
    queries = draw_queries(jax.random.fold_in(jax.random.fold_in(arg_keys[7], part), 71), part)
    keys = draw_keys(jax.random.fold_in(jax.random.fold_in(arg_keys[7], part), 71), part)
    values = normal_values(own_keys[2], (TOKENS, WIDTH), 1.0, 6.0, ((0, 16),))
    out_grad = normal_values(own_keys[3], (TOKENS, WIDTH), 1.0, 6.0, ((0, 16),))
    valid_counts = place_ends(jax.random.randint(own_keys[4], (NROWS, PC), 1, BLK + 1), jax.random.fold_in(own_keys[4], 1), 1, BLK).astype(jnp.int32)
    landmark_cols = place_ends(jax.random.randint(own_keys[5], (NROWS,), 0, PC), jax.random.fold_in(own_keys[5], 1), 0, PC - 1).astype(jnp.int32)
    landmark_rows = draw_landmark_rows(jax.random.fold_in(jax.random.fold_in(arg_keys[7], part), 71), part)
    return dict(queries=queries, keys=keys, values=values, out_grad=out_grad, valid_counts=valid_counts, landmark_cols=landmark_cols, landmark_rows=landmark_rows)


masked_score = -1e+30

def product(form, left, right):
    return jnp.einsum(form, left.astype(jnp.float32), right.astype(jnp.float32), precision=lax.Precision.HIGHEST)

def window_stack(near_rows, columns):
    pieces = [near_rows[row_off, col_off:col_off + columns] for row_off in range(3) for col_off in range(3)]
    stacked = jnp.stack(pieces, axis=1)
    return stacked.reshape(columns, 9 * stacked.shape[2], stacked.shape[3])

def window_mask(count_near, columns, block_len):
    pieces = [count_near[row_off, col_off:col_off + columns] for row_off in range(3) for col_off in range(3)]
    counts = jnp.stack(pieces, axis=1)
    position = jnp.arange(block_len)
    return (position[None, None, :] < counts[:, :, None]).reshape(columns, 9 * block_len)

def spread(grad_window, columns, block_len):
    pieces = grad_window.reshape(columns, 9, block_len, grad_window.shape[-1])
    layers = []
    for row_off in range(3):
        left = jnp.pad(pieces[:, row_off * 3], ((0, 2), (0, 0), (0, 0)))
        middle = jnp.pad(pieces[:, row_off * 3 + 1], ((1, 1), (0, 0), (0, 0)))
        right = jnp.pad(pieces[:, row_off * 3 + 2], ((2, 0), (0, 0), (0, 0)))
        layers.append(left + middle + right)
    return jnp.stack(layers)

def attend(query_blocks, grad_raw, keys_win, values_win, mask_win, keys_land, values_land, mask_land, query_valid):
    score_scale = 1.0 / math.sqrt(query_blocks.shape[-1])
    scores_win = product('cqhe,cwhe->chqw', query_blocks, keys_win) * score_scale
    scores_land = product('cqhe,lhe->chql', query_blocks, keys_land) * score_scale
    scores_win = jnp.where(mask_win[:, None, None, :], scores_win, masked_score)
    scores_land = jnp.where(mask_land[None, None, None, :], scores_land, masked_score)
    row_max = jnp.maximum(lax.optimization_barrier(jnp.max(scores_win, axis=-1)), lax.optimization_barrier(jnp.max(scores_land, axis=-1)))
    exp_total = lax.optimization_barrier(jnp.sum(jnp.exp(scores_win - row_max[..., None]), axis=-1)) + lax.optimization_barrier(jnp.sum(jnp.exp(scores_land - row_max[..., None]), axis=-1))
    log_total = row_max + jnp.log(exp_total)
    probs_win = jnp.exp(scores_win - log_total[..., None])
    probs_land = jnp.exp(scores_land - log_total[..., None])
    low_win = probs_win.astype(jnp.bfloat16)
    low_land = probs_land.astype(jnp.bfloat16)
    mixed_out = product('chqw,cwhe->cqhe', low_win, values_win) + product('chql,lhe->cqhe', low_land, values_land)
    query_mask = query_valid[:, :, None, None]
    attn_part = jnp.where(query_mask, mixed_out, 0.0).astype(jnp.bfloat16)
    grad_in = jnp.where(query_mask, grad_raw, jnp.zeros_like(grad_raw))
    row_delta = lax.optimization_barrier(jnp.sum(grad_in.astype(jnp.float32) * mixed_out, axis=-1))
    row_delta = jnp.transpose(row_delta, (0, 2, 1))[..., None]
    dprob_win = product('cqhe,cwhe->chqw', grad_in, values_win)
    dprob_land = product('cqhe,lhe->chql', grad_in, values_land)
    dscore_win = (probs_win * (dprob_win - row_delta) * score_scale).astype(jnp.bfloat16)
    dscore_land = (probs_land * (dprob_land - row_delta) * score_scale).astype(jnp.bfloat16)
    query_part = (product('chqw,cwhe->cqhe', dscore_win, keys_win) + product('chql,lhe->cqhe', dscore_land, keys_land)).astype(jnp.bfloat16)
    kgrad_win = product('chqw,cqhe->cwhe', dscore_win, query_blocks)
    vgrad_win = product('chqw,cqhe->cwhe', low_win, grad_in)
    kgrad_land = product('chql,cqhe->lhe', dscore_land, query_blocks)
    vgrad_land = product('chql,cqhe->lhe', low_land, grad_in)
    return (attn_part, query_part, kgrad_win, vgrad_win, kgrad_land, vgrad_land)

def reference(queries, keys, values, out_grad, valid_counts, landmark_cols, landmark_rows):
    model_width = HEADS * HD
    key_value = jnp.concatenate([keys, values], axis=1).reshape(NROWS, PC, BLK, 2 * model_width)
    kv_padded = jnp.pad(key_value, ((1, 1), (1, 1), (0, 0), (0, 0)))
    count_padded = jnp.pad(valid_counts, ((1, 1), (1, 1)))
    row_ids = jnp.arange(NROWS, dtype=jnp.int32)
    land_panel = key_value[row_ids, landmark_cols]
    panel_counts = valid_counts[row_ids, landmark_cols]
    query_rows = queries.reshape(NROWS, PC, BLK, HEADS, HD)
    grad_rows = out_grad.reshape(NROWS, PC, BLK, HEADS, HD)
    position = jnp.arange(BLK)

    def row_step(state_pair, row_index):
        window_grads, land_grads = state_pair
        near_rows = lax.dynamic_slice_in_dim(kv_padded, row_index, 3, 0)
        count_near = lax.dynamic_slice_in_dim(count_padded, row_index, 3, 0)
        chosen_rows = landmark_rows[row_index]
        chosen = land_panel[chosen_rows]
        chosen_counts = panel_counts[chosen_rows]
        stacked = window_stack(near_rows, PC)
        keys_win = stacked[..., :model_width].reshape(PC, 9 * BLK, HEADS, HD)
        values_win = stacked[..., model_width:].reshape(PC, 9 * BLK, HEADS, HD)
        mask_win = window_mask(count_near, PC, BLK)
        keys_land = chosen[..., :model_width].reshape(NLAND * BLK, HEADS, HD)
        values_land = chosen[..., model_width:].reshape(NLAND * BLK, HEADS, HD)
        mask_land = (position[None, :] < chosen_counts[:, None]).reshape(NLAND * BLK)
        query_valid = position[None, :] < valid_counts[row_index][:, None]
        attn_part, query_part, kgrad_win, vgrad_win, kgrad_land, vgrad_land = attend(query_rows[row_index], grad_rows[row_index], keys_win, values_win, mask_win, keys_land, values_land, mask_land, query_valid)
        grad_window = jnp.concatenate([kgrad_win.reshape(PC, 9 * BLK, model_width), vgrad_win.reshape(PC, 9 * BLK, model_width)], axis=-1)
        summed = spread(grad_window, PC, BLK)
        current = lax.dynamic_slice_in_dim(window_grads, row_index, 3, 0)
        window_grads = lax.dynamic_update_slice_in_dim(window_grads, current + summed, row_index, 0)
        grad_land = jnp.concatenate([kgrad_land.reshape(NLAND, BLK, model_width), vgrad_land.reshape(NLAND, BLK, model_width)], axis=-1)
        land_grads = land_grads.at[chosen_rows].add(grad_land)
        return ((window_grads, land_grads), (attn_part, query_part))
    start_state = (jnp.zeros((NROWS + 2, PC + 2, BLK, 2 * model_width), jnp.float32), jnp.zeros((NROWS, BLK, 2 * model_width), jnp.float32))
    final_state, row_outputs = lax.scan(row_step, start_state, row_ids)
    window_grads, land_grads = final_state
    attn_rows, qgrad_rows = row_outputs
    all_grads = window_grads[1:-1, 1:-1].at[row_ids, landmark_cols].add(land_grads)
    attn_out = attn_rows.reshape(TOKENS, model_width)
    query_grad = qgrad_rows.reshape(TOKENS, model_width)
    key_grad = all_grads[..., :model_width].astype(jnp.bfloat16).reshape(TOKENS, model_width)
    value_grad = all_grads[..., model_width:].astype(jnp.bfloat16).reshape(TOKENS, model_width)
    return (attn_out, query_grad, key_grad, value_grad)
```

```python
import functools

import jax
import jax.numpy as jnp
from jax import lax
from jax.experimental import pallas as pl
from jax.experimental.pallas import tpu as pltpu
from jax.sharding import PartitionSpec as P

HEADS = 8
HD = 64
BLK = 64
NLAND = 4
PC = 4
WIDTH = HEADS * HD
ROWS = PC * BLK
KEYS = 3 * ROWS + NLAND * BLK
F32 = jnp.float32
BF16 = jnp.bfloat16
MESH = pl.DeviceIdType.MESH
masked_score = -1e30
VMEM_LIMIT = 60 * 1024 * 1024


def dot(a, b):
    return lax.dot_general(a, b, (((1,), (0,)), ((), ())), preferred_element_type=F32)


def remote(src, dst, send, recv, device):
    return pltpu.make_async_remote_copy(
        src_ref=src,
        dst_ref=dst,
        send_sem=send,
        recv_sem=recv,
        device_id={"prow": device},
        device_id_type=MESH,
    )


def position(n):
    me = lax.axis_index("prow")
    z, y, c = me // 4, (me // 2) % 2, me % 2
    core = me + 1 - 2 * c
    side = me + 2 - 4 * y
    return me, z, y, c, core, side


def greet(n):
    me, z, y, c, core, side = position(n)
    last = n // 4 - 1
    other = me + 2 * c - 1
    has_other = jnp.logical_and(other >= 0, other < n)
    barrier = pltpu.get_barrier_semaphore()

    def signal(device):
        pl.semaphore_signal(barrier, inc=1, device_id={"prow": device}, device_id_type=MESH)

    signal(core)
    signal(side)
    pl.when(z > 0)(lambda: signal(me - 4))
    pl.when(z < last)(lambda: signal(me + 4))
    pl.when(has_other)(lambda: signal(other))
    count = (
        2
        + jnp.where(z > 0, 1, 0)
        + jnp.where(z < last, 1, 0)
        + jnp.where(has_other, 1, 0)
    )
    pl.semaphore_wait(barrier, count)


def gather_kernel(
    n,
    cols_ref,
    k_ref,
    v_ref,
    ka,
    va,
    kb,
    vb,
    panel,
    recv,
    up_s,
    dn_s,
    core_s,
    side_s,
    win_s,
    win_r,
):
    me, z, y, c, core, side = position(n)
    depth = n // 4
    last = depth - 1
    half = n // 2
    own_col = cols_ref[me]
    panel[me, :, :WIDTH] = k_ref[own_col]
    panel[me, :, WIDTH:] = v_ref[own_col]

    @pl.when(me == 0)
    def _():
        ka[...] = jnp.zeros_like(ka)
        va[...] = jnp.zeros_like(va)

    @pl.when(me == n - 1)
    def _():
        kb[...] = jnp.zeros_like(kb)
        vb[...] = jnp.zeros_like(vb)

    greet(n)

    def hop(slot, sems, device):
        return remote(panel.at[slot], panel.at[slot], sems.at[slot // 2], recv.at[slot], device)

    to_side = remote(panel.at[me], panel.at[me], side_s.at[0], recv.at[me], side)
    to_side.start()

    def up(slot):
        return hop(slot, up_s, me + 4)

    def down(slot):
        return hop(slot, dn_s, me - 4)

    def over(slot):
        return hop(slot, core_s, core)

    def spread(slot):
        pl.when(z < last)(lambda: up(slot).start())
        pl.when(z > 0)(lambda: down(slot).start())
        over(slot).start()

    spread(me)
    below_k = remote(k_ref, ka, win_s.at[0], win_r.at[0], me + 1)
    below_v = remote(v_ref, va, win_s.at[1], win_r.at[1], me + 1)
    above_k = remote(k_ref, kb, win_s.at[2], win_r.at[2], me - 1)
    above_v = remote(v_ref, vb, win_s.at[3], win_r.at[3], me - 1)

    @pl.when(me < n - 1)
    def _():
        below_k.start()
        below_v.start()

    @pl.when(me > 0)
    def _():
        above_k.start()
        above_v.start()

    hop(side, core_s, core).wait_recv()
    spread(side)
    for s in range(1, depth):
        for flip in range(2):
            row = y + flip * (1 - 2 * y)

            @pl.when(z - s >= 0)
            def _():
                slot = 4 * (z - s) + 2 * row + c
                over(slot).wait_recv()
                pl.when(z < last)(lambda: up(slot).start())
                over(slot).start()

            @pl.when(z + s <= last)
            def _():
                slot = 4 * (z + s) + 2 * row + c
                over(slot).wait_recv()
                pl.when(z > 0)(lambda: down(slot).start())
                over(slot).start()

    for k in range(half):
        over(2 * k + 1 - c).wait_recv()

    @pl.when(me > 0)
    def _():
        below_k.wait_recv()
        below_v.wait_recv()

    @pl.when(me < n - 1)
    def _():
        above_k.wait_recv()
        above_v.wait_recv()

    to_side.wait_send()
    for k in range(half):
        over(2 * k + c).wait_send()
        pl.when(jnp.logical_and(z < last, k // 2 <= z))(lambda: up(2 * k + c).wait_send())
        pl.when(jnp.logical_and(z > 0, k // 2 >= z))(lambda: down(2 * k + c).wait_send())

    @pl.when(me < n - 1)
    def _():
        below_k.wait_send()
        below_v.wait_send()

    @pl.when(me > 0)
    def _():
        above_k.wait_send()
        above_v.wait_send()


def attend_kernel(
    n,
    counts_ref,
    cols_ref,
    rows_ref,
    q_ref,
    do_ref,
    k_ref,
    v_ref,
    ka,
    va,
    kb,
    vb,
    panel,
    attn_ref,
    qgrad_ref,
    g_above,
    g_own,
    g_below,
    g_land,
    k_all,
    v_all,
    k_t,
    v_t,
    q_s,
    do_m,
    q_t,
    do_t,
    o_t,
    dq_t,
    bias,
):
    me = lax.axis_index("prow")
    k_all[0:ROWS] = ka[...]
    k_all[ROWS : 2 * ROWS] = k_ref[...]
    k_all[2 * ROWS : 3 * ROWS] = kb[...]
    v_all[0:ROWS] = va[...]
    v_all[ROWS : 2 * ROWS] = v_ref[...]
    v_all[2 * ROWS : 3 * ROWS] = vb[...]
    pos = lax.broadcasted_iota(jnp.int32, (BLK, ROWS), 0)
    qcol = lax.broadcasted_iota(jnp.int32, (BLK, ROWS), 1) // BLK
    for a in range(3):
        row = me + a - 1
        inside = jnp.logical_and(row >= 0, row < n)
        safe = jnp.clip(row, 0, n - 1)
        for b in range(PC):
            count = jnp.where(inside, counts_ref[safe, b], 0)
            ok = (pos < count) & (qcol >= b - 1) & (qcol <= b + 1)
            base = a * ROWS + b * BLK
            bias[base : base + BLK] = jnp.where(ok, 0.0, masked_score)
    for j in range(NLAND):
        row = rows_ref[0, j]
        count = counts_ref[row, cols_ref[row]]
        base = 3 * ROWS + j * BLK
        bias[base : base + BLK] = jnp.where(pos < count, 0.0, masked_score)
        k_all[base : base + BLK] = panel[row, :, :WIDTH]
        v_all[base : base + BLK] = panel[row, :, WIDTH:]
    k_t[...] = k_all[...].T
    v_t[...] = v_all[...].T
    q_s[...] = q_ref[...] * 0.125
    tpos = lax.broadcasted_iota(jnp.int32, (BLK, WIDTH), 0)
    lane = lax.broadcasted_iota(jnp.int32, (1, ROWS), 1)
    own_valid = jnp.zeros((1, ROWS), jnp.bool_)
    for b in range(PC):
        count = counts_ref[me, b]
        own_valid = own_valid | ((lane >= b * BLK) & (lane < b * BLK + count))
        part = do_ref[b * BLK : (b + 1) * BLK].astype(F32)
        do_m[b * BLK : (b + 1) * BLK] = jnp.where(tpos < count, part, 0.0).astype(BF16)
    q_t[...] = q_s[...].T
    do_t[...] = do_m[...].T
    g_land[NLAND] = jnp.zeros((BLK, 2 * WIDTH), BF16)

    def pair(p, carry):
        cols = pl.ds(pl.multiple_of(p * 128, 128), 128)
        vcols = pl.ds(pl.multiple_of(WIDTH + p * 128, 128), 128)
        k2 = k_all[:, cols]
        v2 = v_all[:, cols]
        q2 = q_s[:, cols]
        do2 = do_m[:, cols]
        zero = jnp.zeros((HD, ROWS), BF16)
        left = lax.broadcasted_iota(jnp.int32, (ROWS, 128), 1) < HD
        dk2 = None
        dv2 = None
        for h in range(2):
            rows = pl.ds(pl.multiple_of(p * 128 + h * HD, HD), HD)
            qt = q_t[rows, :]
            dot_t = do_t[rows, :]
            qt_w = jnp.concatenate([qt, zero] if h == 0 else [zero, qt], axis=0)
            dot_w = jnp.concatenate([dot_t, zero] if h == 0 else [zero, dot_t], axis=0)
            keep = left if h == 0 else jnp.logical_not(left)
            q_w = jnp.where(keep, q2.astype(F32), 0.0).astype(BF16)
            do_w = jnp.where(keep, do2.astype(F32), 0.0).astype(BF16)
            s = dot(k2, qt_w) + bias[...]
            top = jnp.max(s, axis=0, keepdims=True)
            e = jnp.exp(s - top)
            prob = e * (1.0 / jnp.sum(e, axis=0, keepdims=True))
            low = prob.astype(BF16)
            mixed = dot(v_t[rows, :], low)
            o_t[rows, :] = jnp.where(own_valid, mixed, 0.0)
            delta = jnp.sum(dot_t.astype(F32) * mixed, axis=0, keepdims=True)
            dprob = dot(v2, dot_w)
            ds = (prob * (dprob - delta)).astype(BF16)
            dq_t[rows, :] = dot(k_t[rows, :], ds) * 0.125
            dk = dot(ds, q_w)
            dv = dot(low, do_w)
            dk2 = dk if dk2 is None else dk2 + dk
            dv2 = dv if dv2 is None else dv2 + dv
        for part, where in ((dk2, cols), (dv2, vcols)):
            g_above[:, where] = part[0:ROWS].astype(BF16)
            g_own[:, where] = part[ROWS : 2 * ROWS]
            g_below[:, where] = part[2 * ROWS : 3 * ROWS].astype(BF16)
            for j in range(NLAND):
                base = 3 * ROWS + j * BLK
                g_land[j, :, where] = part[base : base + BLK].astype(BF16)
        return carry

    lax.fori_loop(0, HEADS // 2, pair, 0)
    attn_ref[...] = o_t[...].T.astype(BF16)
    qgrad_ref[...] = dq_t[...].T.astype(BF16)


def reduce_kernel(
    n,
    inv_ref,
    hit_ref,
    g_above,
    g_own,
    g_below,
    g_land,
    kgrad_ref,
    vgrad_ref,
    from_below,
    from_above,
    core_tx,
    core_rx,
    acc,
    up_rx,
    dn_rx,
    side_rx,
    core_s,
    core_r,
    hop_s,
    up_r,
    dn_r,
    side_s,
    side_r,
    win_s,
    win_r,
):
    me, z, y, c, core, side = position(n)
    depth = n // 4
    last = depth - 1
    greet(n)

    def over(k):
        return remote(core_tx.at[k], core_rx.at[k], core_s.at[k], core_r.at[k], core)

    def up(k):
        return remote(acc.at[k], up_rx.at[k], hop_s.at[k], up_r.at[k], me + 4)

    def down(k):
        return remote(acc.at[k], dn_rx.at[k], hop_s.at[k], dn_r.at[k], me - 4)

    def give(k):
        core_tx[k] = g_land[inv_ref[2 * k + 1 - c]]
        over(k).start()

    for s in range(depth - 1, -1, -1):
        for row in range(2):
            pl.when(z + s <= last)(lambda: give(2 * (z + s) + row))
            if s > 0:
                pl.when(z - s >= 0)(lambda: give(2 * (z - s) + row))
    to_above = remote(g_above, from_below, win_s.at[0], win_r.at[0], me - 1)
    to_below = remote(g_below, from_above, win_s.at[1], win_r.at[1], me + 1)
    pl.when(me > 0)(lambda: to_above.start())
    pl.when(me < n - 1)(lambda: to_below.start())

    def mine(k):
        over(k).wait_recv()
        return core_rx[k].astype(F32) + g_land[inv_ref[2 * k + c]].astype(F32)

    for s in range(depth - 1, 0, -1):
        for row in range(2):

            @pl.when(z + s <= last)
            def _():
                k = 2 * (z + s) + row
                total = mine(k)

                @pl.when(z > 0)
                def _():
                    up(k).wait_recv()
                    acc[k] = (total + up_rx[k].astype(F32)).astype(BF16)

                @pl.when(z == 0)
                def _():
                    acc[k] = total.astype(BF16)

                up(k).start()

            @pl.when(z - s >= 0)
            def _():
                k = 2 * (z - s) + row
                total = mine(k)

                @pl.when(z < last)
                def _():
                    down(k).wait_recv()
                    acc[k] = (total + dn_rx[k].astype(F32)).astype(BF16)

                @pl.when(z == last)
                def _():
                    acc[k] = total.astype(BF16)

                down(k).start()

    def arrived(k):
        pl.when(z > 0)(lambda: up(k).wait_recv())
        pl.when(z < last)(lambda: down(k).wait_recv())
        low = jnp.where(z > 0, up_rx[k].astype(F32), 0.0)
        high = jnp.where(z < last, dn_rx[k].astype(F32), 0.0)
        return mine(k) + low + high

    @pl.when(z == 0)
    def _():
        for row in range(2):
            up_rx[row] = jnp.zeros((BLK, 2 * WIDTH), BF16)

    @pl.when(z == last)
    def _():
        for row in range(2):
            dn_rx[2 * last + row] = jnp.zeros((BLK, 2 * WIDTH), BF16)

    theirs = 2 * z + 1 - y
    acc[theirs] = arrived(theirs).astype(BF16)
    to_side = remote(acc.at[theirs], side_rx, side_s.at[0], side_r.at[0], side)
    to_side.start()
    total = arrived(2 * z + y)

    @pl.when(me == n - 1)
    def _():
        from_below[...] = jnp.zeros_like(from_below)

    @pl.when(me == 0)
    def _():
        from_above[...] = jnp.zeros_like(from_above)

    pl.when(me < n - 1)(lambda: to_above.wait_recv())
    pl.when(me > 0)(lambda: to_below.wait_recv())
    to_side.wait_recv()
    total = total + side_rx[...].astype(F32)
    for b in range(PC):
        span = pl.ds(b * BLK, BLK)
        part = (
            g_own[span, :]
            + from_above[span, :].astype(F32)
            + from_below[span, :].astype(F32)
            + jnp.where(hit_ref[0] == b, total, 0.0)
        ).astype(BF16)
        kgrad_ref[span, :] = part[:, :WIDTH]
        vgrad_ref[span, :] = part[:, WIDTH:]
    to_side.wait_send()
    pl.when(me > 0)(lambda: to_above.wait_send())
    pl.when(me < n - 1)(lambda: to_below.wait_send())
    for k in range(n // 2):
        over(k).wait_send()
        pl.when(k // 2 > z)(lambda: up(k).wait_send())
        pl.when(k // 2 < z)(lambda: down(k).wait_send())


VM = pl.BlockSpec(memory_space=pltpu.VMEM)
SM = pl.BlockSpec(memory_space=pltpu.SMEM)
DMA = pltpu.SemaphoreType.DMA


def shape(dims, dtype):
    return jax.ShapeDtypeStruct(dims, dtype)


def per_device(n, queries, keys, values, out_grad, valid_counts, landmark_cols, landmark_rows):
    half = n // 2
    block_rows = (PC, BLK, WIDTH)
    k4 = keys.reshape(block_rows)
    v4 = values.reshape(block_rows)
    ka, va, kb, vb, panel = pl.pallas_call(
        functools.partial(gather_kernel, n),
        out_shape=[shape(block_rows, BF16)] * 4 + [shape((n, BLK, 2 * WIDTH), BF16)],
        in_specs=[SM, VM, VM],
        out_specs=[VM] * 5,
        scratch_shapes=[
            DMA((n,)),
            DMA((half,)),
            DMA((half,)),
            DMA((half,)),
            DMA((1,)),
            DMA((4,)),
            DMA((4,)),
        ],
        compiler_params=pltpu.CompilerParams(
            collective_id=0, has_side_effects=True, vmem_limit_bytes=VMEM_LIMIT
        ),
    )(landmark_cols, k4, v4)
    flat = (ROWS, WIDTH)
    attn_out, query_grad, g_above, g_own, g_below, g_land = pl.pallas_call(
        functools.partial(attend_kernel, n),
        out_shape=[
            shape(flat, BF16),
            shape(flat, BF16),
            shape((ROWS, 2 * WIDTH), BF16),
            shape((ROWS, 2 * WIDTH), F32),
            shape((ROWS, 2 * WIDTH), BF16),
            shape((NLAND + 1, BLK, 2 * WIDTH), BF16),
        ],
        in_specs=[SM] * 3 + [VM] * 9,
        out_specs=[VM] * 6,
        scratch_shapes=[
            pltpu.VMEM((KEYS, WIDTH), BF16),
            pltpu.VMEM((KEYS, WIDTH), BF16),
            pltpu.VMEM((WIDTH, KEYS), BF16),
            pltpu.VMEM((WIDTH, KEYS), BF16),
            pltpu.VMEM((ROWS, WIDTH), BF16),
            pltpu.VMEM((ROWS, WIDTH), BF16),
            pltpu.VMEM((WIDTH, ROWS), BF16),
            pltpu.VMEM((WIDTH, ROWS), BF16),
            pltpu.VMEM((WIDTH, ROWS), F32),
            pltpu.VMEM((WIDTH, ROWS), F32),
            pltpu.VMEM((KEYS, ROWS), F32),
        ],
        compiler_params=pltpu.CompilerParams(vmem_limit_bytes=VMEM_LIMIT),
    )(
        valid_counts,
        landmark_cols,
        landmark_rows,
        queries,
        out_grad,
        keys,
        values,
        ka.reshape(flat),
        va.reshape(flat),
        kb.reshape(flat),
        vb.reshape(flat),
        panel,
    )
    match = landmark_rows[0][None, :] == jnp.arange(n, dtype=jnp.int32)[:, None]
    slots = jnp.arange(NLAND, dtype=jnp.int32)[None, :] - NLAND
    inverse = NLAND + jnp.sum(jnp.where(match, slots, 0), axis=1)
    hit = lax.dynamic_slice_in_dim(landmark_cols, lax.axis_index("prow"), 1, 0)
    block = (BLK, 2 * WIDTH)
    many = pltpu.VMEM((half,) + block, BF16)
    key_grad, value_grad = pl.pallas_call(
        functools.partial(reduce_kernel, n),
        out_shape=[shape(flat, BF16)] * 2,
        in_specs=[SM] * 2 + [VM] * 4,
        out_specs=[VM] * 2,
        scratch_shapes=[
            pltpu.VMEM((ROWS, 2 * WIDTH), BF16),
            pltpu.VMEM((ROWS, 2 * WIDTH), BF16),
            many,
            many,
            many,
            many,
            many,
            pltpu.VMEM(block, BF16),
            DMA((half,)),
            DMA((half,)),
            DMA((half,)),
            DMA((half,)),
            DMA((half,)),
            DMA((1,)),
            DMA((1,)),
            DMA((2,)),
            DMA((2,)),
        ],
        compiler_params=pltpu.CompilerParams(
            collective_id=1, has_side_effects=True, vmem_limit_bytes=VMEM_LIMIT
        ),
    )(inverse, hit, g_above, g_own, g_below, g_land)
    return attn_out, query_grad, key_grad, value_grad


def solution(mesh):
    n = mesh.shape["prow"]
    tokens = P(("chars", "prow"), None)
    return jax.shard_map(
        functools.partial(per_device, n),
        mesh=mesh,
        in_specs=(tokens, tokens, tokens, tokens, P("chars", None), P("chars"), tokens),
        out_specs=(tokens, tokens, tokens, tokens),
        check_vma=False,
    )
```

```python
import functools

import jax
import jax.numpy as jnp
from jax import lax
from jax.experimental import pallas as pl
from jax.experimental.pallas import tpu as pltpu
from jax.sharding import PartitionSpec as P

HEADS = 8
HD = 64
BLK = 64
NLAND = 4
PC = 4
WIDTH = HEADS * HD
ROWS = PC * BLK
KEYS = 3 * ROWS + NLAND * BLK
F32 = jnp.float32
BF16 = jnp.bfloat16
MESH = pl.DeviceIdType.MESH
masked_score = -1e30
WIN = 3 * ROWS
VMEM_LIMIT = 60 * 1024 * 1024


def dot(a, b):
    return lax.dot_general(a, b, (((1,), (0,)), ((), ())), preferred_element_type=F32)


def remote(src, dst, send, recv, device):
    return pltpu.make_async_remote_copy(
        src_ref=src,
        dst_ref=dst,
        send_sem=send,
        recv_sem=recv,
        device_id={"prow": device},
        device_id_type=MESH,
    )


def position(n):
    me = lax.axis_index("prow")
    z, y, c = me // 4, (me // 2) % 2, me % 2
    core = me + 1 - 2 * c
    side = me + 2 - 4 * y
    return me, z, y, c, core, side


def greet(n):
    me, z, y, c, core, side = position(n)
    last = n // 4 - 1
    other = me + 2 * c - 1
    has_other = jnp.logical_and(other >= 0, other < n)
    barrier = pltpu.get_barrier_semaphore()

    def signal(device):
        pl.semaphore_signal(barrier, inc=1, device_id={"prow": device}, device_id_type=MESH)

    signal(core)
    signal(side)
    pl.when(z > 0)(lambda: signal(me - 4))
    pl.when(z < last)(lambda: signal(me + 4))
    pl.when(has_other)(lambda: signal(other))
    count = (
        2
        + jnp.where(z > 0, 1, 0)
        + jnp.where(z < last, 1, 0)
        + jnp.where(has_other, 1, 0)
    )
    pl.semaphore_wait(barrier, count)


def fused_kernel(
    n,
    cols_ref,
    rows_ref,
    counts_ref,
    q_ref,
    k_ref,
    v_ref,
    do_ref,
    attn_ref,
    qgrad_ref,
    kgrad_ref,
    vgrad_ref,
    panel,
    ka,
    va,
    kb,
    vb,
    k_all,
    v_all,
    k_t,
    v_t,
    q_s,
    do_m,
    q_t,
    do_t,
    o_t,
    dq_t,
    bias,
    e_win,
    top_win,
    sum_win,
    low_win,
    ds_win,
    g_above,
    g_own,
    g_below,
    from_below,
    from_above,
    g_land,
    core_tx,
    core_rx,
    up_rx,
    dn_rx,
    side_rx,
    total_ref,
    recv,
    up_s,
    dn_s,
    core_s,
    side_s,
    win_s,
    win_r,
    r_core_s,
    r_core_r,
    r_hop_s,
    r_up_r,
    r_dn_r,
    r_side_s,
    r_side_r,
    r_win_s,
    r_win_r,
):
    me, z, y, c, core, side = position(n)
    depth = n // 4
    last = depth - 1
    half = n // 2
    own_col = cols_ref[me]
    panel[me, :, :WIDTH] = k_ref[own_col]
    panel[me, :, WIDTH:] = v_ref[own_col]

    @pl.when(me == 0)
    def _():
        ka[...] = jnp.zeros_like(ka)
        va[...] = jnp.zeros_like(va)
        from_above[...] = jnp.zeros_like(from_above)

    @pl.when(me == n - 1)
    def _():
        kb[...] = jnp.zeros_like(kb)
        vb[...] = jnp.zeros_like(vb)
        from_below[...] = jnp.zeros_like(from_below)

    greet(n)

    def hop(slot, sems, device):
        return remote(panel.at[slot], panel.at[slot], sems.at[slot // 2], recv.at[slot], device)

    def up(slot):
        return hop(slot, up_s, me + 4)

    def down(slot):
        return hop(slot, dn_s, me - 4)

    def over(slot):
        return hop(slot, core_s, core)

    def spread(slot):
        pl.when(z < last)(lambda: up(slot).start())
        pl.when(z > 0)(lambda: down(slot).start())
        over(slot).start()

    to_side = remote(panel.at[me], panel.at[me], side_s.at[0], recv.at[me], side)
    to_side.start()
    spread(me)
    below_k = remote(k_ref, ka, win_s.at[0], win_r.at[0], me + 1)
    below_v = remote(v_ref, va, win_s.at[1], win_r.at[1], me + 1)
    above_k = remote(k_ref, kb, win_s.at[2], win_r.at[2], me - 1)
    above_v = remote(v_ref, vb, win_s.at[3], win_r.at[3], me - 1)

    @pl.when(me < n - 1)
    def _():
        below_k.start()

    @pl.when(me > 0)
    def _():
        above_k.start()

    @pl.when(me < n - 1)
    def _():
        below_v.start()

    @pl.when(me > 0)
    def _():
        above_v.start()

    pos = lax.broadcasted_iota(jnp.int32, (BLK, ROWS), 0)
    qcol = lax.broadcasted_iota(jnp.int32, (BLK, ROWS), 1) // BLK

    for a in range(3):
        row = me + a - 1
        inside = jnp.logical_and(row >= 0, row < n)
        safe = jnp.clip(row, 0, n - 1)
        for b in range(PC):
            count = jnp.where(inside, counts_ref[safe, b], 0)
            ok = (pos < count) & (qcol >= b - 1) & (qcol <= b + 1)
            base = a * ROWS + b * BLK
            bias[base : base + BLK] = jnp.where(ok, 0.0, masked_score)
    for j in range(NLAND):
        row = rows_ref[0, j]
        count = counts_ref[row, cols_ref[row]]
        base = WIN + j * BLK
        bias[base : base + BLK] = jnp.where(pos < count, 0.0, masked_score)
    q_s[...] = q_ref[...] * 0.125
    tpos = lax.broadcasted_iota(jnp.int32, (BLK, WIDTH), 0)
    for b in range(PC):
        part = do_ref[b * BLK : (b + 1) * BLK].astype(F32)
        do_m[b * BLK : (b + 1) * BLK] = jnp.where(tpos < counts_ref[me, b], part, 0.0).astype(BF16)
    q_t[...] = q_s[...].T
    do_t[...] = do_m[...].T
    for g in range(2):
        g_land[g, NLAND] = jnp.zeros((BLK, WIDTH), BF16)

    def own_part(lo, hi, k_rows, v_rows):
        k_rows = k_rows.reshape(hi - lo, WIDTH)
        v_rows = v_rows.reshape(hi - lo, WIDTH)
        k_all[lo:hi] = k_rows
        v_all[lo:hi] = v_rows
        k_t[:, lo:hi] = k_rows.T
        v_t[:, lo:hi] = v_rows.T

    own_part(ROWS, 2 * ROWS, k_ref[...], v_ref[...])

    hop(side, core_s, core).wait_recv()
    spread(side)

    def chain(s):
        for flip in range(2):
            row = y + flip * (1 - 2 * y)

            @pl.when(z - s >= 0)
            def _():
                slot = 4 * (z - s) + 2 * row + c
                over(slot).wait_recv()
                pl.when(z < last)(lambda: up(slot).start())
                over(slot).start()

            @pl.when(z + s <= last)
            def _():
                slot = 4 * (z + s) + 2 * row + c
                over(slot).wait_recv()
                pl.when(z > 0)(lambda: down(slot).start())
                over(slot).start()

    for s in range(1, last):
        chain(s)

    @pl.when(me > 0)
    def _():
        below_k.wait_recv()
        below_v.wait_recv()

    @pl.when(me < n - 1)
    def _():
        above_k.wait_recv()
        above_v.wait_recv()

    own_part(0, ROWS, ka[...], va[...])
    own_part(2 * ROWS, WIN, kb[...], vb[...])
    zero = jnp.zeros((HD, ROWS), BF16)

    def padded(rows_t, h):
        return jnp.concatenate([rows_t, zero] if h == 0 else [zero, rows_t], axis=0)

    def head_rows(p, h):
        return pl.ds(pl.multiple_of(p * 128 + h * HD, HD), HD)

    def pair_cols(p):
        return pl.ds(pl.multiple_of(p * 128, 128), 128)

    def window_scores(p, carry):
        k2 = k_all[0:WIN, pair_cols(p)]
        for h in range(2):
            s = dot(k2, padded(q_t[head_rows(p, h), :], h)) + bias[0:WIN]
            top = jnp.max(s, axis=0, keepdims=True)
            e = jnp.exp(s - top)
            e_win[2 * p + h] = e
            top_win[2 * p + h] = top
            sum_win[2 * p + h] = jnp.sum(e, axis=0, keepdims=True)
        return carry

    lax.fori_loop(0, HEADS // 2, window_scores, 0)
    if last > 0:
        chain(last)
    for k in range(half):
        over(2 * k + 1 - c).wait_recv()
    for j in range(NLAND):
        row = rows_ref[0, j]
        block = panel[row]
        own_part(WIN + j * BLK, WIN + (j + 1) * BLK, block[:, :WIDTH], block[:, WIDTH:])

    left = lax.broadcasted_iota(jnp.int32, (ROWS, 128), 1) < HD

    def halved(block, h):
        keep = left if h == 0 else jnp.logical_not(left)
        return jnp.where(keep, block.astype(F32), 0.0).astype(BF16)

    def landmarks(g, i):
        p = 2 * g + i
        k2 = k_all[WIN:KEYS, pair_cols(p)]
        v2 = v_all[:, pair_cols(p)]
        q2 = q_s[:, pair_cols(p)]
        do2 = do_m[:, pair_cols(p)]
        dk2 = 0.0
        dv2 = 0.0
        for h in range(2):
            rows = head_rows(p, h)
            head = 2 * p + h
            s = dot(k2, padded(q_t[rows, :], h)) + bias[WIN:KEYS]
            top_w = top_win[head]
            top = jnp.maximum(jnp.max(s, axis=0, keepdims=True), top_w)
            e = jnp.exp(s - top)
            scale_w = jnp.exp(top_w - top)
            inv_total = 1.0 / (jnp.sum(e, axis=0, keepdims=True) + sum_win[head] * scale_w)
            prob_l = e * inv_total
            prob_w = e_win[head] * (scale_w * inv_total)
            low_l = prob_l.astype(BF16)
            low_w = prob_w.astype(BF16)
            low_win[head] = low_w
            mixed = dot(v_t[rows, 0:WIN], low_w) + dot(v_t[rows, WIN:KEYS], low_l)
            o_t[rows, :] = mixed
            dot_t = do_t[rows, :]
            delta = jnp.sum(dot_t.astype(F32) * mixed, axis=0, keepdims=True)
            dot_w = padded(dot_t, h)
            ds_l = (prob_l * (dot(v2[WIN:KEYS], dot_w) - delta)).astype(BF16)
            ds_w = (prob_w * (dot(v2[0:WIN], dot_w) - delta)).astype(BF16)
            ds_win[head] = ds_w
            dq_t[rows, :] = (dot(k_t[rows, 0:WIN], ds_w) + dot(k_t[rows, WIN:KEYS], ds_l)) * 0.125
            dk2 = dk2 + dot(ds_l, halved(q2, h))
            dv2 = dv2 + dot(low_l, halved(do2, h))
        for j in range(NLAND):
            span = slice(j * BLK, (j + 1) * BLK)
            g_land[g, j, :, i * 128 : (i + 1) * 128] = dk2[span].astype(BF16)
            g_land[g, j, :, 256 + i * 128 : 256 + (i + 1) * 128] = dv2[span].astype(BF16)

    def slot_of(device):
        found = NLAND
        for j in range(NLAND):
            found = jnp.where(rows_ref[0, j] == device, j, found)
        return found

    def r_over(g, k):
        return remote(
            core_tx.at[g, k], core_rx.at[g, k], r_core_s.at[g, k], r_core_r.at[g, k], core
        )

    def r_up(g, k):
        return remote(core_rx.at[g, k], up_rx.at[g, k], r_hop_s.at[g, k], r_up_r.at[g, k], me + 4)

    def r_down(g, k):
        return remote(core_rx.at[g, k], dn_rx.at[g, k], r_hop_s.at[g, k], r_dn_r.at[g, k], me - 4)

    def give(g, k):
        core_tx[g, k] = g_land[g, slot_of(2 * k + 1 - c)]
        r_over(g, k).start()

    def give_all(g):
        for s in range(last, -1, -1):
            for row in range(2):
                pl.when(z + s <= last)(lambda: give(g, 2 * (z + s) + row))
                if s > 0:
                    pl.when(z - s >= 0)(lambda: give(g, 2 * (z - s) + row))

    def mine(g, k):
        r_over(g, k).wait_recv()
        return core_rx[g, k].astype(F32) + g_land[g, slot_of(2 * k + c)].astype(F32)

    def reduce_step(g, s):
        for row in range(2):

            @pl.when(z + s <= last)
            def _():
                k = 2 * (z + s) + row
                total = mine(g, k)

                @pl.when(z > 0)
                def _():
                    r_up(g, k).wait_recv()
                    core_rx[g, k] = (total + up_rx[g, k].astype(F32)).astype(BF16)

                @pl.when(z == 0)
                def _():
                    core_rx[g, k] = total.astype(BF16)

                r_up(g, k).start()

            @pl.when(z - s >= 0)
            def _():
                k = 2 * (z - s) + row
                total = mine(g, k)

                @pl.when(z < last)
                def _():
                    r_down(g, k).wait_recv()
                    core_rx[g, k] = (total + dn_rx[g, k].astype(F32)).astype(BF16)

                @pl.when(z == last)
                def _():
                    core_rx[g, k] = total.astype(BF16)

                r_down(g, k).start()

    def to_above(p):
        return remote(g_above.at[p], from_below.at[p], r_win_s.at[0, p], r_win_r.at[0, p], me - 1)

    def to_below(p):
        return remote(g_below.at[p], from_above.at[p], r_win_s.at[1, p], r_win_r.at[1, p], me + 1)

    def window_grads(p):
        q2 = q_s[:, p * 128 : (p + 1) * 128]
        do2 = do_m[:, p * 128 : (p + 1) * 128]
        dk2 = dot(ds_win[2 * p], halved(q2, 0)) + dot(ds_win[2 * p + 1], halved(q2, 1))
        dv2 = dot(low_win[2 * p], halved(do2, 0)) + dot(low_win[2 * p + 1], halved(do2, 1))
        for part, cols in ((dk2, slice(0, 128)), (dv2, slice(128, 256))):
            g_above[p, :, cols] = part[0:ROWS].astype(BF16)
            g_own[p, :, cols] = part[ROWS : 2 * ROWS]
            g_below[p, :, cols] = part[2 * ROWS : WIN].astype(BF16)
        pl.when(me > 0)(lambda: to_above(p).start())
        pl.when(me < n - 1)(lambda: to_below(p).start())

    for g in range(2):
        for i in range(2):
            landmarks(g, i)
        give_all(g)
    steps = [(g, s) for s in range(last, 0, -1) for g in range(2)]
    for at in range(max(len(steps), HEADS // 2)):
        if at < HEADS // 2:
            window_grads(at)
        if at < len(steps):
            reduce_step(*steps[at])

    lane = lax.broadcasted_iota(jnp.int32, (1, ROWS), 1)
    own_valid = jnp.zeros((1, ROWS), jnp.bool_)
    for b in range(PC):
        own_valid = own_valid | ((lane >= b * BLK) & (lane < b * BLK + counts_ref[me, b]))
    attn_ref[...] = jnp.where(own_valid, o_t[...], 0.0).T.astype(BF16)
    qgrad_ref[...] = dq_t[...].T.astype(BF16)

    @pl.when(z == 0)
    def _():
        for g in range(2):
            for row in range(2):
                up_rx[g, row] = jnp.zeros((BLK, WIDTH), BF16)

    @pl.when(z == last)
    def _():
        for g in range(2):
            for row in range(2):
                dn_rx[g, 2 * last + row] = jnp.zeros((BLK, WIDTH), BF16)

    def arrived(g, k):
        pl.when(z > 0)(lambda: r_up(g, k).wait_recv())
        pl.when(z < last)(lambda: r_down(g, k).wait_recv())
        return mine(g, k) + up_rx[g, k].astype(F32) + dn_rx[g, k].astype(F32)

    theirs = 2 * z + 1 - y

    def r_side(g):
        return remote(
            core_rx.at[g, theirs], side_rx.at[g], r_side_s.at[g], r_side_r.at[g], side
        )

    for g in range(2):
        core_rx[g, theirs] = arrived(g, theirs).astype(BF16)
        r_side(g).start()
    for g in range(2):
        total_ref[g] = arrived(g, 2 * z + y)
    for p in range(HEADS // 2):
        pl.when(me < n - 1)(lambda: to_above(p).wait_recv())
        pl.when(me > 0)(lambda: to_below(p).wait_recv())
    for g in range(2):
        r_side(g).wait_recv()
        total_ref[g] = total_ref[g] + side_rx[g].astype(F32)
    for p in range(HEADS // 2):
        g, i = p // 2, p % 2
        for b in range(PC):
            span = slice(b * BLK, (b + 1) * BLK)
            hit = own_col == b
            for out, cols, base in (
                (kgrad_ref, slice(0, 128), i * 128),
                (vgrad_ref, slice(128, 256), 256 + i * 128),
            ):
                out[span, p * 128 : (p + 1) * 128] = (
                    g_own[p, span, cols]
                    + from_above[p, span, cols].astype(F32)
                    + from_below[p, span, cols].astype(F32)
                    + jnp.where(hit, total_ref[g, :, base : base + 128], 0.0)
                ).astype(BF16)

    to_side.wait_send()
    for k in range(half):
        slot = 2 * k + c
        over(slot).wait_send()
        pl.when(jnp.logical_and(z < last, k // 2 <= z))(lambda: up(slot).wait_send())
        pl.when(jnp.logical_and(z > 0, k // 2 >= z))(lambda: down(slot).wait_send())
        for g in range(2):
            r_over(g, k).wait_send()
            pl.when(k // 2 > z)(lambda: r_up(g, k).wait_send())
            pl.when(k // 2 < z)(lambda: r_down(g, k).wait_send())
    for g in range(2):
        r_side(g).wait_send()

    @pl.when(me < n - 1)
    def _():
        below_k.wait_send()
        below_v.wait_send()
        for p in range(HEADS // 2):
            to_below(p).wait_send()

    @pl.when(me > 0)
    def _():
        above_k.wait_send()
        above_v.wait_send()
        for p in range(HEADS // 2):
            to_above(p).wait_send()


def emit_kernel(*refs):
    sems = refs[-1]
    copies = [pltpu.make_async_copy(refs[i], refs[4 + i], sems.at[i]) for i in range(4)]
    for copy in copies:
        copy.start()
    for copy in copies:
        copy.wait()


VM = pl.BlockSpec(memory_space=pltpu.VMEM)
SM = pl.BlockSpec(memory_space=pltpu.SMEM)
ANY = pl.BlockSpec(memory_space=pl.ANY)
DMA = pltpu.SemaphoreType.DMA


def shape(dims, dtype):
    return jax.ShapeDtypeStruct(dims, dtype)


def per_device(n, queries, keys, values, out_grad, valid_counts, landmark_cols, landmark_rows):
    half = n // 2
    flat = (ROWS, WIDTH)
    block_rows = (PC, BLK, WIDTH)
    flat_t = (WIDTH, ROWS)
    pairs = (HEADS // 2, ROWS, 256)
    halves = (2, half, BLK, WIDTH)
    vmem = pltpu.VMEM
    results = pl.pallas_call(
        functools.partial(fused_kernel, n),
        out_shape=[shape(flat, BF16)] * 4,
        in_specs=[SM] * 3 + [VM] * 4,
        out_specs=[VM] * 4,
        scratch_shapes=[
            vmem((n, BLK, 2 * WIDTH), BF16),
            vmem(block_rows, BF16),
            vmem(block_rows, BF16),
            vmem(block_rows, BF16),
            vmem(block_rows, BF16),
            vmem((KEYS, WIDTH), BF16),
            vmem((KEYS, WIDTH), BF16),
            vmem((WIDTH, KEYS), BF16),
            vmem((WIDTH, KEYS), BF16),
            vmem(flat, BF16),
            vmem(flat, BF16),
            vmem(flat_t, BF16),
            vmem(flat_t, BF16),
            vmem(flat_t, F32),
            vmem(flat_t, F32),
            vmem((KEYS, ROWS), F32),
            vmem((HEADS, WIN, ROWS), F32),
            vmem((HEADS, 1, ROWS), F32),
            vmem((HEADS, 1, ROWS), F32),
            vmem((HEADS, WIN, ROWS), BF16),
            vmem((HEADS, WIN, ROWS), BF16),
            vmem(pairs, BF16),
            vmem(pairs, F32),
            vmem(pairs, BF16),
            vmem(pairs, BF16),
            vmem(pairs, BF16),
            vmem((2, NLAND + 1, BLK, WIDTH), BF16),
            vmem(halves, BF16),
            vmem(halves, BF16),
            vmem(halves, BF16),
            vmem(halves, BF16),
            vmem((2, BLK, WIDTH), BF16),
            vmem((2, BLK, WIDTH), F32),
            DMA((n,)),
            DMA((half,)),
            DMA((half,)),
            DMA((half,)),
            DMA((1,)),
            DMA((4,)),
            DMA((4,)),
            DMA((2, half)),
            DMA((2, half)),
            DMA((2, half)),
            DMA((2, half)),
            DMA((2, half)),
            DMA((2,)),
            DMA((2,)),
            DMA((2, HEADS // 2)),
            DMA((2, HEADS // 2)),
        ],
        compiler_params=pltpu.CompilerParams(
            collective_id=0, has_side_effects=True, vmem_limit_bytes=VMEM_LIMIT
        ),
    )(
        landmark_cols,
        landmark_rows,
        valid_counts,
        queries,
        keys.reshape(block_rows),
        values.reshape(block_rows),
        out_grad,
    )
    return tuple(
        pl.pallas_call(
            emit_kernel,
            out_shape=[shape(flat, BF16)] * 4,
            in_specs=[ANY] * 4,
            out_specs=[ANY] * 4,
            scratch_shapes=[DMA((4,))],
        )(*results)
    )


def solution(mesh):
    n = mesh.shape["prow"]
    tokens = P(("chars", "prow"), None)
    return jax.shard_map(
        functools.partial(per_device, n),
        mesh=mesh,
        in_specs=(tokens, tokens, tokens, tokens, P("chars", None), P("chars"), tokens),
        out_specs=(tokens, tokens, tokens, tokens),
        check_vma=False,
    )
```

```python
import functools

import jax
import jax.numpy as jnp
from jax import lax
from jax.experimental import pallas as pl
from jax.experimental.pallas import tpu as pltpu
from jax.sharding import PartitionSpec as P

HEADS = 8
HD = 64
BLK = 64
NLAND = 4
PC = 4
WIDTH = HEADS * HD
ROWS = PC * BLK
KEYS = 3 * ROWS + NLAND * BLK
F32 = jnp.float32
BF16 = jnp.bfloat16
MESH = pl.DeviceIdType.MESH
masked_score = -1e30
WIN = 3 * ROWS
VMEM_LIMIT = 60 * 1024 * 1024


def dot(a, b):
    return lax.dot_general(a, b, (((1,), (0,)), ((), ())), preferred_element_type=F32)


def remote(src, dst, send, recv, device):
    return pltpu.make_async_remote_copy(
        src_ref=src,
        dst_ref=dst,
        send_sem=send,
        recv_sem=recv,
        device_id={"prow": device},
        device_id_type=MESH,
    )


def position(n):
    me = lax.axis_index("prow")
    z, y, c = me // 4, (me // 2) % 2, me % 2
    core = me + 1 - 2 * c
    side = me + 2 - 4 * y
    return me, z, y, c, core, side


def greet(n):
    me, z, y, c, core, side = position(n)
    last = n // 4 - 1
    other = me + 2 * c - 1
    has_other = jnp.logical_and(other >= 0, other < n)
    barrier = pltpu.get_barrier_semaphore()

    def signal(device):
        pl.semaphore_signal(barrier, inc=1, device_id={"prow": device}, device_id_type=MESH)

    signal(core)
    signal(side)
    pl.when(z > 0)(lambda: signal(me - 4))
    pl.when(z < last)(lambda: signal(me + 4))
    pl.when(has_other)(lambda: signal(other))
    count = (
        2
        + jnp.where(z > 0, 1, 0)
        + jnp.where(z < last, 1, 0)
        + jnp.where(has_other, 1, 0)
    )
    pl.semaphore_wait(barrier, count)


def fused_kernel(
    n,
    cols_ref,
    rows_ref,
    counts_ref,
    q_ref,
    k_ref,
    v_ref,
    do_ref,
    attn_ref,
    qgrad_ref,
    kgrad_ref,
    vgrad_ref,
    panel,
    ka,
    va,
    kb,
    vb,
    k_all,
    v_all,
    k_t,
    v_t,
    q_s,
    do_m,
    q_t,
    do_t,
    o_t,
    dq_t,
    bias,
    e_win,
    top_win,
    sum_win,
    low_win,
    ds_win,
    g_above,
    g_own,
    g_below,
    from_below,
    from_above,
    g_land,
    core_tx,
    core_rx,
    up_rx,
    dn_rx,
    side_rx,
    total_ref,
    recv,
    up_s,
    dn_s,
    core_s,
    side_s,
    win_s,
    win_r,
    r_core_s,
    r_core_r,
    r_hop_s,
    r_up_r,
    r_dn_r,
    r_side_s,
    r_side_r,
    r_win_s,
    r_win_r,
):
    me, z, y, c, core, side = position(n)
    depth = n // 4
    last = depth - 1
    half = n // 2
    own_col = cols_ref[me]
    panel[me, :, :WIDTH] = k_ref[own_col]
    panel[me, :, WIDTH:] = v_ref[own_col]

    @pl.when(me == 0)
    def _():
        ka[...] = jnp.zeros_like(ka)
        va[...] = jnp.zeros_like(va)
        from_above[...] = jnp.zeros_like(from_above)

    @pl.when(me == n - 1)
    def _():
        kb[...] = jnp.zeros_like(kb)
        vb[...] = jnp.zeros_like(vb)
        from_below[...] = jnp.zeros_like(from_below)

    greet(n)

    def hop(slot, sems, device):
        return remote(panel.at[slot], panel.at[slot], sems.at[slot // 2], recv.at[slot], device)

    def up(slot):
        return hop(slot, up_s, me + 4)

    def down(slot):
        return hop(slot, dn_s, me - 4)

    def over(slot):
        return hop(slot, core_s, core)

    def spread(slot):
        pl.when(z < last)(lambda: up(slot).start())
        pl.when(z > 0)(lambda: down(slot).start())
        over(slot).start()

    to_side = remote(panel.at[me], panel.at[me], side_s.at[0], recv.at[me], side)
    to_side.start()
    spread(me)
    below_k = remote(k_ref, ka, win_s.at[0], win_r.at[0], me + 1)
    below_v = remote(v_ref, va, win_s.at[1], win_r.at[1], me + 1)
    above_k = remote(k_ref, kb, win_s.at[2], win_r.at[2], me - 1)
    above_v = remote(v_ref, vb, win_s.at[3], win_r.at[3], me - 1)

    @pl.when(me < n - 1)
    def _():
        below_k.start()

    @pl.when(me > 0)
    def _():
        above_k.start()

    @pl.when(me < n - 1)
    def _():
        below_v.start()

    @pl.when(me > 0)
    def _():
        above_v.start()

    pos = lax.broadcasted_iota(jnp.int32, (BLK, ROWS), 0)
    qcol = lax.broadcasted_iota(jnp.int32, (BLK, ROWS), 1) // BLK

    for a in range(3):
        row = me + a - 1
        inside = jnp.logical_and(row >= 0, row < n)
        safe = jnp.clip(row, 0, n - 1)
        for b in range(PC):
            count = jnp.where(inside, counts_ref[safe, b], 0)
            ok = (pos < count) & (qcol >= b - 1) & (qcol <= b + 1)
            base = a * ROWS + b * BLK
            bias[base : base + BLK] = jnp.where(ok, 0.0, masked_score)
    for j in range(NLAND):
        row = rows_ref[0, j]
        count = counts_ref[row, cols_ref[row]]
        base = WIN + j * BLK
        bias[base : base + BLK] = jnp.where(pos < count, 0.0, masked_score)
    q_s[...] = q_ref[...] * 0.125
    tpos = lax.broadcasted_iota(jnp.int32, (BLK, WIDTH), 0)
    for b in range(PC):
        part = do_ref[b * BLK : (b + 1) * BLK].astype(F32)
        do_m[b * BLK : (b + 1) * BLK] = jnp.where(tpos < counts_ref[me, b], part, 0.0).astype(BF16)
    q_t[...] = q_s[...].T
    do_t[...] = do_m[...].T
    for g in range(2):
        g_land[g, NLAND] = jnp.zeros((BLK, WIDTH), BF16)

    def own_part(lo, hi, k_rows, v_rows):
        k_rows = k_rows.reshape(hi - lo, WIDTH)
        v_rows = v_rows.reshape(hi - lo, WIDTH)
        k_all[lo:hi] = k_rows
        v_all[lo:hi] = v_rows
        k_t[:, lo:hi] = k_rows.T
        v_t[:, lo:hi] = v_rows.T

    own_part(ROWS, 2 * ROWS, k_ref[...], v_ref[...])

    hop(side, core_s, core).wait_recv()
    spread(side)

    def chain(s):
        for flip in range(2):
            row = y + flip * (1 - 2 * y)

            @pl.when(z - s >= 0)
            def _():
                slot = 4 * (z - s) + 2 * row + c
                over(slot).wait_recv()
                pl.when(z < last)(lambda: up(slot).start())
                over(slot).start()

            @pl.when(z + s <= last)
            def _():
                slot = 4 * (z + s) + 2 * row + c
                over(slot).wait_recv()
                pl.when(z > 0)(lambda: down(slot).start())
                over(slot).start()

    for s in range(1, last):
        chain(s)

    @pl.when(me > 0)
    def _():
        below_k.wait_recv()
        below_v.wait_recv()

    @pl.when(me < n - 1)
    def _():
        above_k.wait_recv()
        above_v.wait_recv()

    own_part(0, ROWS, ka[...], va[...])
    own_part(2 * ROWS, WIN, kb[...], vb[...])
    zero = jnp.zeros((HD, ROWS), BF16)

    def padded(rows_t, h):
        return jnp.concatenate([rows_t, zero] if h == 0 else [zero, rows_t], axis=0)

    def head_rows(p, h):
        return pl.ds(pl.multiple_of(p * 128 + h * HD, HD), HD)

    def pair_cols(p):
        return pl.ds(pl.multiple_of(p * 128, 128), 128)

    def window_scores(p, carry):
        k2 = k_all[0:WIN, pair_cols(p)]
        for h in range(2):
            s = dot(k2, padded(q_t[head_rows(p, h), :], h)) + bias[0:WIN]
            top = jnp.max(s, axis=0, keepdims=True)
            e = jnp.exp(s - top)
            e_win[2 * p + h] = e
            top_win[2 * p + h] = top
            sum_win[2 * p + h] = jnp.sum(e, axis=0, keepdims=True)
        return carry

    lax.fori_loop(0, HEADS // 2, window_scores, 0)
    if last > 0:
        chain(last)
    for k in range(half):
        over(2 * k + 1 - c).wait_recv()
    for j in range(NLAND):
        row = rows_ref[0, j]
        block = panel[row]
        own_part(WIN + j * BLK, WIN + (j + 1) * BLK, block[:, :WIDTH], block[:, WIDTH:])

    left = lax.broadcasted_iota(jnp.int32, (ROWS, 128), 1) < HD

    def halved(block, h):
        keep = left if h == 0 else jnp.logical_not(left)
        return jnp.where(keep, block.astype(F32), 0.0).astype(BF16)

    def landmarks(g, i):
        p = 2 * g + i
        k2 = k_all[WIN:KEYS, pair_cols(p)]
        v2 = v_all[:, pair_cols(p)]
        q2 = q_s[:, pair_cols(p)]
        do2 = do_m[:, pair_cols(p)]
        dk2 = 0.0
        dv2 = 0.0
        for h in range(2):
            rows = head_rows(p, h)
            head = 2 * p + h
            s = dot(k2, padded(q_t[rows, :], h)) + bias[WIN:KEYS]
            top_w = top_win[head]
            top = jnp.maximum(jnp.max(s, axis=0, keepdims=True), top_w)
            e = jnp.exp(s - top)
            scale_w = jnp.exp(top_w - top)
            inv_total = 1.0 / (jnp.sum(e, axis=0, keepdims=True) + sum_win[head] * scale_w)
            prob_l = e * inv_total
            prob_w = e_win[head] * (scale_w * inv_total)
            low_l = prob_l.astype(BF16)
            low_w = prob_w.astype(BF16)
            low_win[head] = low_w
            mixed = dot(v_t[rows, 0:WIN], low_w) + dot(v_t[rows, WIN:KEYS], low_l)
            o_t[rows, :] = mixed
            dot_t = do_t[rows, :]
            delta = jnp.sum(dot_t.astype(F32) * mixed, axis=0, keepdims=True)
            dot_w = padded(dot_t, h)
            ds_l = (prob_l * (dot(v2[WIN:KEYS], dot_w) - delta)).astype(BF16)
            ds_w = (prob_w * (dot(v2[0:WIN], dot_w) - delta)).astype(BF16)
            ds_win[head] = ds_w
            dq_t[rows, :] = (dot(k_t[rows, 0:WIN], ds_w) + dot(k_t[rows, WIN:KEYS], ds_l)) * 0.125
            dk2 = dk2 + dot(ds_l, halved(q2, h))
            dv2 = dv2 + dot(low_l, halved(do2, h))
        for j in range(NLAND):
            span = slice(j * BLK, (j + 1) * BLK)
            g_land[g, j, :, i * 128 : (i + 1) * 128] = dk2[span].astype(BF16)
            g_land[g, j, :, 256 + i * 128 : 256 + (i + 1) * 128] = dv2[span].astype(BF16)

    def slot_of(device):
        found = NLAND
        for j in range(NLAND):
            found = jnp.where(rows_ref[0, j] == device, j, found)
        return found

    def r_over(g, k):
        return remote(
            core_tx.at[g, k], core_rx.at[g, k], r_core_s.at[g, k], r_core_r.at[g, k], core
        )

    def r_up(g, k):
        return remote(core_rx.at[g, k], up_rx.at[g, k], r_hop_s.at[g, k], r_up_r.at[g, k], me + 4)

    def r_down(g, k):
        return remote(core_rx.at[g, k], dn_rx.at[g, k], r_hop_s.at[g, k], r_dn_r.at[g, k], me - 4)

    def give(g, k):
        core_tx[g, k] = g_land[g, slot_of(2 * k + 1 - c)]
        r_over(g, k).start()

    def give_all(g):
        for s in range(last, -1, -1):
            for row in range(2):
                pl.when(z + s <= last)(lambda: give(g, 2 * (z + s) + row))
                if s > 0:
                    pl.when(z - s >= 0)(lambda: give(g, 2 * (z - s) + row))

    def mine(g, k):
        r_over(g, k).wait_recv()
        return core_rx[g, k].astype(F32) + g_land[g, slot_of(2 * k + c)].astype(F32)

    def reduce_step(g, s):
        for row in range(2):

            @pl.when(z + s <= last)
            def _():
                k = 2 * (z + s) + row
                total = mine(g, k)

                @pl.when(z > 0)
                def _():
                    r_up(g, k).wait_recv()
                    core_rx[g, k] = (total + up_rx[g, k].astype(F32)).astype(BF16)

                @pl.when(z == 0)
                def _():
                    core_rx[g, k] = total.astype(BF16)

                r_up(g, k).start()

            @pl.when(z - s >= 0)
            def _():
                k = 2 * (z - s) + row
                total = mine(g, k)

                @pl.when(z < last)
                def _():
                    r_down(g, k).wait_recv()
                    core_rx[g, k] = (total + dn_rx[g, k].astype(F32)).astype(BF16)

                @pl.when(z == last)
                def _():
                    core_rx[g, k] = total.astype(BF16)

                r_down(g, k).start()

    def to_above(p):
        return remote(g_above.at[p], from_below.at[p], r_win_s.at[0, p], r_win_r.at[0, p], me - 1)

    def to_below(p):
        return remote(g_below.at[p], from_above.at[p], r_win_s.at[1, p], r_win_r.at[1, p], me + 1)

    def window_grads(p):
        q2 = q_s[:, p * 128 : (p + 1) * 128]
        do2 = do_m[:, p * 128 : (p + 1) * 128]
        dk2 = dot(ds_win[2 * p], halved(q2, 0)) + dot(ds_win[2 * p + 1], halved(q2, 1))
        dv2 = dot(low_win[2 * p], halved(do2, 0)) + dot(low_win[2 * p + 1], halved(do2, 1))
        for part, cols in ((dk2, slice(0, 128)), (dv2, slice(128, 256))):
            g_above[p, :, cols] = part[0:ROWS].astype(BF16)
            g_own[p, :, cols] = part[ROWS : 2 * ROWS]
            g_below[p, :, cols] = part[2 * ROWS : WIN].astype(BF16)
        pl.when(me > 0)(lambda: to_above(p).start())
        pl.when(me < n - 1)(lambda: to_below(p).start())

    for g in range(2):
        for i in range(2):
            landmarks(g, i)
        give_all(g)
    steps = [(g, s) for s in range(last, 0, -1) for g in range(2)]
    for at in range(max(len(steps), HEADS // 2)):
        if at < HEADS // 2:
            window_grads(at)
        if at < len(steps):
            reduce_step(*steps[at])

    lane = lax.broadcasted_iota(jnp.int32, (1, ROWS), 1)
    own_valid = jnp.zeros((1, ROWS), jnp.bool_)
    for b in range(PC):
        own_valid = own_valid | ((lane >= b * BLK) & (lane < b * BLK + counts_ref[me, b]))
    attn_ref[...] = jnp.where(own_valid, o_t[...], 0.0).T.astype(BF16)
    qgrad_ref[...] = dq_t[...].T.astype(BF16)

    @pl.when(z == 0)
    def _():
        for g in range(2):
            for row in range(2):
                up_rx[g, row] = jnp.zeros((BLK, WIDTH), BF16)

    @pl.when(z == last)
    def _():
        for g in range(2):
            for row in range(2):
                dn_rx[g, 2 * last + row] = jnp.zeros((BLK, WIDTH), BF16)

    def arrived(g, k):
        pl.when(z > 0)(lambda: r_up(g, k).wait_recv())
        pl.when(z < last)(lambda: r_down(g, k).wait_recv())
        return mine(g, k) + up_rx[g, k].astype(F32) + dn_rx[g, k].astype(F32)

    theirs = 2 * z + 1 - y

    def r_side(g):
        return remote(
            core_rx.at[g, theirs], side_rx.at[g], r_side_s.at[g], r_side_r.at[g], side
        )

    for g in range(2):
        core_rx[g, theirs] = arrived(g, theirs).astype(BF16)
        r_side(g).start()
    for g in range(2):
        total_ref[g] = arrived(g, 2 * z + y)
    for p in range(HEADS // 2):
        pl.when(me < n - 1)(lambda: to_above(p).wait_recv())
        pl.when(me > 0)(lambda: to_below(p).wait_recv())
    for g in range(2):
        r_side(g).wait_recv()
        total_ref[g] = total_ref[g] + side_rx[g].astype(F32)
    for p in range(HEADS // 2):
        g, i = p // 2, p % 2
        for b in range(PC):
            span = slice(b * BLK, (b + 1) * BLK)
            hit = own_col == b
            for out, cols, base in (
                (kgrad_ref, slice(0, 128), i * 128),
                (vgrad_ref, slice(128, 256), 256 + i * 128),
            ):
                out[span, p * 128 : (p + 1) * 128] = (
                    g_own[p, span, cols]
                    + from_above[p, span, cols].astype(F32)
                    + from_below[p, span, cols].astype(F32)
                    + jnp.where(hit, total_ref[g, :, base : base + 128], 0.0)
                ).astype(BF16)

    to_side.wait_send()
    for k in range(half):
        slot = 2 * k + c
        over(slot).wait_send()
        pl.when(jnp.logical_and(z < last, k // 2 <= z))(lambda: up(slot).wait_send())
        pl.when(jnp.logical_and(z > 0, k // 2 >= z))(lambda: down(slot).wait_send())
        for g in range(2):
            r_over(g, k).wait_send()
            pl.when(k // 2 > z)(lambda: r_up(g, k).wait_send())
            pl.when(k // 2 < z)(lambda: r_down(g, k).wait_send())
    for g in range(2):
        r_side(g).wait_send()

    @pl.when(me < n - 1)
    def _():
        below_k.wait_send()
        below_v.wait_send()
        for p in range(HEADS // 2):
            to_below(p).wait_send()

    @pl.when(me > 0)
    def _():
        above_k.wait_send()
        above_v.wait_send()
        for p in range(HEADS // 2):
            to_above(p).wait_send()


def emit_kernel(*refs):
    for source, result in zip(refs[:4], refs[4:]):
        result[...] = source[...]


VM = pl.BlockSpec(memory_space=pltpu.VMEM)
SM = pl.BlockSpec(memory_space=pltpu.SMEM)
DMA = pltpu.SemaphoreType.DMA


def shape(dims, dtype):
    return jax.ShapeDtypeStruct(dims, dtype)


def per_device(n, queries, keys, values, out_grad, valid_counts, landmark_cols, landmark_rows):
    half = n // 2
    flat = (ROWS, WIDTH)
    block_rows = (PC, BLK, WIDTH)
    flat_t = (WIDTH, ROWS)
    pairs = (HEADS // 2, ROWS, 256)
    halves = (2, half, BLK, WIDTH)
    vmem = pltpu.VMEM
    results = pl.pallas_call(
        functools.partial(fused_kernel, n),
        out_shape=[shape(flat, BF16)] * 4,
        in_specs=[SM] * 3 + [VM] * 4,
        out_specs=[VM] * 4,
        scratch_shapes=[
            vmem((n, BLK, 2 * WIDTH), BF16),
            vmem(block_rows, BF16),
            vmem(block_rows, BF16),
            vmem(block_rows, BF16),
            vmem(block_rows, BF16),
            vmem((KEYS, WIDTH), BF16),
            vmem((KEYS, WIDTH), BF16),
            vmem((WIDTH, KEYS), BF16),
            vmem((WIDTH, KEYS), BF16),
            vmem(flat, BF16),
            vmem(flat, BF16),
            vmem(flat_t, BF16),
            vmem(flat_t, BF16),
            vmem(flat_t, F32),
            vmem(flat_t, F32),
            vmem((KEYS, ROWS), F32),
            vmem((HEADS, WIN, ROWS), F32),
            vmem((HEADS, 1, ROWS), F32),
            vmem((HEADS, 1, ROWS), F32),
            vmem((HEADS, WIN, ROWS), BF16),
            vmem((HEADS, WIN, ROWS), BF16),
            vmem(pairs, BF16),
            vmem(pairs, F32),
            vmem(pairs, BF16),
            vmem(pairs, BF16),
            vmem(pairs, BF16),
            vmem((2, NLAND + 1, BLK, WIDTH), BF16),
            vmem(halves, BF16),
            vmem(halves, BF16),
            vmem(halves, BF16),
            vmem(halves, BF16),
            vmem((2, BLK, WIDTH), BF16),
            vmem((2, BLK, WIDTH), F32),
            DMA((n,)),
            DMA((half,)),
            DMA((half,)),
            DMA((half,)),
            DMA((1,)),
            DMA((4,)),
            DMA((4,)),
            DMA((2, half)),
            DMA((2, half)),
            DMA((2, half)),
            DMA((2, half)),
            DMA((2, half)),
            DMA((2,)),
            DMA((2,)),
            DMA((2, HEADS // 2)),
            DMA((2, HEADS // 2)),
        ],
        compiler_params=pltpu.CompilerParams(
            collective_id=0, has_side_effects=True, vmem_limit_bytes=VMEM_LIMIT
        ),
    )(
        landmark_cols,
        landmark_rows,
        valid_counts,
        queries,
        keys.reshape(block_rows),
        values.reshape(block_rows),
        out_grad,
    )
    return tuple(
        pl.pallas_call(
            emit_kernel,
            out_shape=[shape(flat, BF16)] * 4,
            in_specs=[VM] * 4,
            out_specs=[VM] * 4,
        )(*results)
    )


def solution(mesh):
    n = mesh.shape["prow"]
    tokens = P(("chars", "prow"), None)
    return jax.shard_map(
        functools.partial(per_device, n),
        mesh=mesh,
        in_specs=(tokens, tokens, tokens, tokens, P("chars", None), P("chars"), tokens),
        out_specs=(tokens, tokens, tokens, tokens),
        check_vma=False,
    )
```
